512 devices in a mesh: vocab: 64 (over y, x, core), width: 8 (over z).
Axes of the slice: x: 4, y: 8, z: 8, core: 2. Of those that a mesh axis runs over, the one named last changes fastest.
Arguments:
- hidden: bfloat16 [8192, 2048], P('vocab', 'width'), may hold values from -400 to 400
- norm_gain: bfloat16 [2048], P('width'), may hold values from 0.5 to 1.5
- head_weight: bfloat16 [102400, 2048], P('vocab', 'width'), may hold values from -1 to 1
- targets: int32 [8192], P(('vocab', 'width')), may hold values from 0 to 102399
- pad_mask: int32 [8192], P(('vocab', 'width')), may hold values 0 or 1
- lengths: int32 [64], replicated, may hold values from 1 to 2048, 8192 in all
Outputs:
- entropy: float32 [8192], P(('vocab', 'width'))
- token_logprob: float32 [8192], P(('vocab', 'width'))
- seq_score: float32 [64], replicated
The draws below stay inside these ranges and needn't reach their ends.
Inputs may be any that keep to these rules, and one draw needn't show every extreme that they name: The lengths sum to 8192.
All inputs are finite; a program needn't handle non-finite values. No bound on the sum of `pad_mask` on one device may be relied on, other than what follows from the above.
Results may differ from the reference program's by a relative error of at most 0.0031.
Values may be sent and summed in bfloat16 or wider, within the bound.
A program may use at most 64 MiB of HBM per device.

```python
import math
import jax
import jax.numpy as jnp
import numpy as np
from jax import lax

D = 2048
VOCAB = 102400
NSEQ = 64
TOKENS = 8192


def draw_head_weight(key, part):
    weight_scale = 3.5 / math.sqrt(D)
    values = jax.random.truncated_normal(jax.random.fold_in(key, 1), -4.0, 4.0, (VOCAB, D), jnp.float32) * weight_scale
    return values.astype(jnp.bfloat16)


def draw_hidden(key, part):
    key_rows, key_cols, key_vals = jax.random.split(jax.random.fold_in(key, 2), 3)
    row_scale = jnp.exp(jax.random.uniform(key_rows, (TOKENS, 1), jnp.float32, 0.0, math.log(10.0)))
    col_scale = jnp.exp(jax.random.uniform(key_cols, (1, D), jnp.float32, 0.0, math.log(10.0)))
    values = jax.random.truncated_normal(key_vals, -4.0, 4.0, (TOKENS, D), jnp.float32)
    values = values * row_scale * col_scale
    return values.astype(jnp.bfloat16)


def set_ends(array, stream_key, low, largest):
    longest = array.shape.index(max(array.shape))
    spots = []
    for shift in (0, 1):
        where = [jax.random.randint(jax.random.fold_in(stream_key, axis), (), 0, length) for axis, length in enumerate(array.shape)]
        where[longest] = (where[longest] + shift) % array.shape[longest]
        spots.append(tuple(where))
    return array.at[spots[0]].set(low).at[spots[1]].set(largest)


def ranked_wide(key, shape, count, skew):
    loads = [min(1 << octave, count + 1 - (1 << octave)) * (1 << 20) // math.isqrt((1 << octave) ** skew) + 1 for octave in range((count + 1).bit_length()) if 1 << octave <= count]
    deviation = 1 + sum(loads) // (1 << 30)
    listing = np.cumsum(np.array([max(1, weight // deviation) for weight in loads]))
    ticket = jax.random.randint(jax.random.fold_in(key, 1), shape, 0, int(listing[len(loads) - 1]))
    start = jnp.left_shift(1, jnp.searchsorted(jnp.asarray(listing, jnp.int32), ticket, side="right").astype(jnp.int32))
    grade = start - 1 + jax.random.randint(jax.random.fold_in(key, 4), shape, 0, 1 << 30) % jnp.minimum(start, count + 1 - start)
    return jax.random.permutation(jax.random.fold_in(key, 2), count)[grade].astype(jnp.int32)


def length_profile(amount, total, limit, skew):
    portions = [(1 << 20) // math.isqrt(standing ** skew) + 1 for standing in range(2, amount + 1)]
    spare, counts = total - limit - (amount - 1), [1] * (amount - 1)
    while spare > 0:
        candidates = [i for i in range(amount - 1) if counts[i] < limit]
        pool, budget = sum([portions[i] for i in candidates]), spare
        for i in candidates:
            addition = min(limit - counts[i], max(1, budget * portions[i] // pool), spare)
            counts[i] = counts[i] + addition
            spare = spare - addition
    return np.array([limit] + counts)


def uneven(key, amount, total, most, lean):
    if amount == 2:
        one = jax.random.randint(key, (), max(1, total - most), min(most, total - 1) + 1)
        return jnp.stack([one, total - one])
    tallies = jnp.asarray(length_profile(amount, total, most, lean), jnp.int32)
    twos = (amount - 1) // 2
    donor, sink = tallies[1:1 + 2 * twos:2], tallies[2:2 + 2 * twos:2]
    margin = jnp.minimum(donor - 1, most - sink)
    moved = jax.random.randint(jax.random.fold_in(key, 1), (twos,), 0, 1 << 20) % (margin + 1)
    tallies = tallies.at[1:1 + 2 * twos:2].set(donor - moved).at[2:2 + 2 * twos:2].set(sink + moved)
    return tallies[jax.random.permutation(jax.random.fold_in(key, 2), amount)]


def setup_inputs(seed: int = 0) -> dict:
    streams_of = jax.random.split(jax.random.key(seed), 7)
    return {
        "hidden": draw_hidden(jax.random.fold_in(streams_of[6], 71), 0),
        "norm_gain": jnp.clip(1.0 + 0.1 * jax.random.normal(streams_of[1], (D,), jnp.float32), 0.5, 1.5).astype(jnp.bfloat16),
        "head_weight": draw_head_weight(jax.random.fold_in(streams_of[6], 71), 0),
        "targets": set_ends(ranked_wide(streams_of[3], (TOKENS,), VOCAB, 2), jax.random.fold_in(streams_of[3], 3), 0, VOCAB - 1).astype(jnp.int32),
        "pad_mask": set_ends((jax.random.randint(streams_of[4], (TOKENS,), 0, 4) < 3).astype(jnp.int32), jax.random.fold_in(streams_of[4], 1), 0, 1),
        "lengths": uneven(streams_of[5], NSEQ, TOKENS, TOKENS // 4, 2).astype(jnp.int32),
    }


epsilon = 1e-06

def reference(hidden, norm_gain, head_weight, targets, pad_mask, lengths):
    values = hidden.astype(jnp.float32)
    mean_square = lax.optimization_barrier(jnp.mean(values * values, axis=1))
    normed = (values * lax.rsqrt(mean_square + epsilon)[:, None] * norm_gain.astype(jnp.float32)[None, :]).astype(jnp.bfloat16)
    head_float = head_weight.astype(jnp.float32)
    block_rows = math.gcd(TOKENS, 512)

    def per_block(inputs):
        block_normed, block_ids = inputs
        logits = jnp.dot(block_normed.astype(jnp.float32), head_float.T, precision=lax.Precision.HIGHEST)
        peak = lax.optimization_barrier(jnp.max(logits, axis=1))
        shifted = logits - peak[:, None]
        weights = jnp.exp(shifted)
        exp_total = lax.optimization_barrier(jnp.sum(weights, axis=1))
        spread = lax.optimization_barrier(jnp.sum(weights * shifted, axis=1))
        target_logit = jnp.take_along_axis(logits, block_ids[:, None].astype(jnp.int32), axis=1)[:, 0]
        return (peak, exp_total, spread, target_logit)
    peak, exp_total, spread, target_logit = lax.map(per_block, (normed.reshape(-1, block_rows, D), targets.reshape(-1, block_rows)))
    peak = peak.reshape(-1)
    exp_total = exp_total.reshape(-1)
    spread = spread.reshape(-1)
    target_logit = target_logit.reshape(-1)
    kept_mask = pad_mask.astype(jnp.float32)
    log_total = jnp.log(exp_total)
    entropy = kept_mask * (log_total - spread / exp_total)
    token_logprob = kept_mask * (target_logit - peak - log_total)
    seq_ends = jnp.cumsum(lengths).astype(jnp.int32)
    seq_starts = seq_ends - lengths.astype(jnp.int32)
    token_index = jnp.arange(TOKENS, dtype=jnp.int32)
    member = ((token_index[:, None] >= seq_starts[None, :]) & (token_index[:, None] < seq_ends[None, :])).astype(jnp.float32)
    seq_score = lax.optimization_barrier(jnp.sum(member * token_logprob[:, None], axis=0)) / lengths.astype(jnp.float32)
    return (entropy, token_logprob, seq_score)
```

```python
import functools

import jax
import jax.numpy as jnp
from jax import lax
from jax.experimental import pallas as pl
from jax.experimental.pallas import tpu as pltpu
from jax.sharding import PartitionSpec as P

epsilon = 1e-06
MESH = pl.DeviceIdType.MESH
NX, NY, NC, NZ = 4, 8, 2, 8
GROUP = NC * NX
F32 = jnp.float32
NT = (((1,), (1,)), ((), ()))


def remote(src, dst, send, recv, device):
    return pltpu.make_async_remote_copy(
        src_ref=src, dst_ref=dst, send_sem=send, recv_sem=recv, device_id=device, device_id_type=MESH
    )


def merge_tiles(tiles):
    peak = functools.reduce(jnp.maximum, [t[0:1] for t in tiles])
    total = spread = target = None
    for t in tiles:
        gap = t[0:1] - peak
        lift = jnp.exp(gap)
        parts = (t[1:2] * lift, lift * (t[2:3] + gap * t[1:2]), t[3:4])
        if total is None:
            total, spread, target = parts
        else:
            total, spread, target = total + parts[0], spread + parts[1], target + parts[2]
    return peak, total, spread, target


def stack_rows(*rows):
    return jnp.concatenate(rows + (jnp.zeros((8 - len(rows), rows[0].shape[1]), F32),), axis=0)


def kernel(
    packed, digits, head, bounds, final, seq,
    raw, toks, heads, acc, stats, got_y, got_c, sum_z, sum_y,
    az_s, az_r, h_s, h_r, x_s, x_r, y_s, y_r, c_s, c_r, t_s, t_r,
):
    v = lax.axis_index("vocab")
    w = lax.axis_index("width")
    core = v % NC
    x = (v // NC) % NX
    y = v // (NC * NX)
    mine = core * NX + x
    rows, wide = head.shape
    ways, parts = 2, 2
    piece = rows // (ways * parts)

    def at_z(d):
        return {"width": (w + d) % NZ}

    def at_y(d):
        return {"vocab": (((y + d) % NY) * NX + x) * NC + core}

    def at_c(d):
        other = (mine + d) % GROUP
        return {"vocab": (y * NX + other % NX) * NC + other // NX}

    def at_x(d):
        return {"vocab": (y * NX + (x + d) % NX) * NC + core}

    barrier = pltpu.get_barrier_semaphore()
    for d in range(1, 8):
        for device in (at_z(d), at_y(d), at_c(d)):
            pl.semaphore_signal(barrier, inc=1, device_id=device, device_id_type=MESH)
    pl.semaphore_wait(barrier, 21)

    sent = []
    for d in range(1, NZ):
        copy = remote(packed.at[(w + d) % NZ], raw.at[w], az_s.at[d - 1], az_r.at[d - 1], at_z(d))
        copy.start()
        sent.append(copy)

    def head_copy(step, way, part):
        span = pl.ds((way * parts + part) * piece, piece)
        owner = (w - step + NZ) % NZ if way == 0 else (w + step) % NZ
        src = head.at[span] if step == 0 else heads.at[owner, span]
        return remote(
            src, heads.at[owner, span], h_s.at[way, step, part], h_r.at[way, step, part],
            at_z(1 if way == 0 else NZ - 1),
        )

    ring = {}

    def head_step(step):
        for part in range(parts):
            for way in range(ways):
                if step > 0:
                    ring[step - 1, way, part].wait_recv()
                if step < NZ - 1:
                    copy = head_copy(step, way, part)
                    copy.start()
                    ring[step, way, part] = copy

    head_step(0)
    raw[w] = packed[w]
    acc[...] = jnp.zeros_like(acc)
    for copy in sent:
        copy.wait_recv()

    values = raw[:, 0:16, :].astype(F32)
    gain = raw[:, 16:32, :].astype(F32)
    energy = jnp.sum(jnp.sum(values * values, axis=0), axis=1, keepdims=True)
    inv = lax.rsqrt(energy / (wide * NZ) + epsilon)
    toks[y, mine, 0:NZ] = (values * inv[None] * gain).astype(jnp.bfloat16)
    toks[y, mine, NZ] = digits[...]

    spot = toks.at[y, mine]
    xs = []
    for d in range(1, NX):
        copy = remote(spot, spot, x_s.at[d - 1], x_r.at[d - 1], at_x(d))
        copy.start()
        xs.append(copy)
    for copy in xs:
        copy.wait_recv()

    yring = {}

    def y_step(step):
        for way, hops in ((0, NY // 2), (1, NY // 2 - 1)):
            if 0 < step <= hops:
                yring[step - 1, way].wait_recv()
            if step < hops:
                owner = (y - step + NY) % NY if way == 0 else (y + step) % NY
                block = toks.at[owner, pl.ds(core * NX, NX)]
                copy = remote(
                    block, block, y_s.at[way, step], y_r.at[way, step], at_y(1 if way == 0 else NY - 1)
                )
                copy.start()
                yring[step, way] = copy

    y_step(0)
    for step in range(1, NY // 2 + 1):
        head_step(step)
        y_step(step)
    side = toks.at[:, pl.ds(core * NX, NX)]
    cross = remote(side, side, c_s.at[0], c_r.at[0], {"vocab": v - core + (1 - core)})
    cross.start()

    half = rows // ways

    def multiply(near, far):
        def one(i, carry):
            step = near + i // 4
            tile = i % 4
            lanes = pl.ds(pl.multiple_of(tile * 256, 256), 256)
            for way in range(ways):
                owner = (w - step + NZ) % NZ if way == 0 else (w + step) % NZ
                tokens = toks[pl.ds(tile * 2, 2), :, owner].reshape(256, wide)
                block = heads[owner, pl.ds(way * half, half)]
                span = pl.ds(way * half, half)
                acc[span, lanes] += lax.dot_general(block, tokens, NT, preferred_element_type=F32)
            return carry

        lax.fori_loop(0, (far - near) * 4, one, 0)

    heads[w] = head[...]
    head_step(5)
    cross.wait_recv()
    multiply(0, 3)
    head_step(6)
    multiply(3, 7)
    head_step(7)
    multiply(7, 8)

    chunk = rows // 10
    pick = (
        lax.broadcasted_iota(jnp.int32, (8, 256), 0) == lax.broadcasted_iota(jnp.int32, (8, 256), 1)
    ).astype(jnp.bfloat16)

    def side_values(block):
        return lax.dot_general(pick, block.reshape(128, 256), NT, preferred_element_type=F32)

    def fold(values, op):
        return op(values.reshape(chunk // 8, 8, 128), axis=0)

    def summarize(tile, carry):
        lanes = pl.ds(pl.multiple_of(tile * 128, 128), 128)
        extra = side_values(toks[tile, :, NZ])
        wanted = extra[0:1] * 4096.0 + extra[1:2] * 64.0 + extra[2:3] - (v * rows).astype(F32)
        wanted = wanted.astype(jnp.int32)

        def top(i, peak):
            return jnp.maximum(peak, fold(acc[pl.ds(i * chunk, chunk), lanes], jnp.max))

        peak = lax.fori_loop(1, 10, top, fold(acc[pl.ds(0, chunk), lanes], jnp.max))
        peak = jnp.max(peak, axis=0, keepdims=True)

        def add(i, sums):
            logits = acc[pl.ds(i * chunk, chunk), lanes]
            shifted = logits - peak
            weights = jnp.exp(shifted)
            place = lax.broadcasted_iota(jnp.int32, (chunk, 128), 0) + i * chunk
            hit = jnp.where(place == wanted, logits, 0.0)
            return (
                sums[0] + fold(weights, jnp.sum),
                sums[1] + fold(weights * shifted, jnp.sum),
                sums[2] + fold(hit, jnp.sum),
            )

        none = jnp.zeros((8, 128), F32)
        sums = lax.fori_loop(0, 10, add, (none, none, none))
        sums = [jnp.sum(s, axis=0, keepdims=True) for s in sums]
        stats[tile] = stack_rows(peak, *sums)
        return carry

    lax.fori_loop(0, NY, summarize, 0)

    def swap(stage, buffer, own, at, source=None):
        copies = []
        for d in range(1, 8):
            src = buffer.at[own] if source is None else source((own + d) % 8)
            copy = remote(src, buffer.at[own], t_s.at[stage, d - 1], t_r.at[stage, d - 1], at(d))
            copy.start()
            copies.append(copy)
        for copy in copies:
            copy.wait_recv()
        return copies

    done = []
    got_y[y] = stats[y]
    done += swap(0, got_y, y, at_y, lambda i: stats.at[i])
    got_c[mine] = stack_rows(*merge_tiles([got_y[i] for i in range(8)]))
    done += swap(1, got_c, mine, at_c)
    peak, total, spread, target = merge_tiles([got_c[i] for i in range(8)])

    kept = side_values(toks[y, :, NZ])[3:4]
    log_total = jnp.log(total)
    entropy = kept * (log_total - spread / total)
    logprob = kept * (target - peak - log_total)
    final[...] = stack_rows(entropy, logprob)

    lane = lax.broadcasted_iota(jnp.int32, (128, 128), 1)
    slot = lane // 16
    token = ((((y * NX + slot % NX) * NC + slot // NX) * NZ) + w) * 16 + lane % 16
    member = ((token >= bounds[0]) & (token < bounds[1])).astype(F32)
    sum_z[w] = lax.dot_general(
        stack_rows(logprob), member, NT, precision=lax.Precision.HIGHEST, preferred_element_type=F32
    )
    done += swap(2, sum_z, w, at_z)
    sum_y[y] = functools.reduce(jnp.add, [sum_z[i] for i in range(8)])
    done += swap(3, sum_y, y, at_y)
    seq[...] = functools.reduce(jnp.add, [sum_y[i] for i in range(8)])

    for copy in sent + xs + [cross] + done + list(yring.values()) + list(ring.values()):
        copy.wait_send()


def per_device(hidden, norm_gain, head_weight, targets, pad_mask, lengths):
    rows, wide = head_weight.shape
    packed = jnp.concatenate(
        [hidden.reshape(NZ, 16, wide), jnp.broadcast_to(norm_gain[None, None], (NZ, 16, wide))], axis=1
    )
    columns = jnp.stack([targets // 4096, (targets // 64) % 64, targets % 64, pad_mask], axis=1)
    digits = jnp.pad(columns.astype(jnp.bfloat16), ((0, 0), (0, wide - 4)))
    seq_ends = jnp.cumsum(lengths)
    bounds = jnp.pad(jnp.stack([seq_ends - lengths, seq_ends]), ((0, 0), (0, 128 - lengths.shape[0])))
    bounds = jnp.broadcast_to(bounds[:, :, None], (2, 128, 128))
    vmem = pl.BlockSpec(memory_space=pltpu.VMEM)
    dma = pltpu.SemaphoreType.DMA
    bf = jnp.bfloat16
    final, seq = pl.pallas_call(
        kernel,
        out_shape=(jax.ShapeDtypeStruct((8, 128), F32), jax.ShapeDtypeStruct((8, 128), F32)),
        in_specs=[vmem] * 4,
        out_specs=(vmem, vmem),
        scratch_shapes=[
            pltpu.VMEM((NZ, 32, wide), bf),
            pltpu.VMEM((NY, GROUP, NZ + 1, 16, wide), bf),
            pltpu.VMEM((NZ, rows, wide), bf),
            pltpu.VMEM((rows, 1024), F32),
            pltpu.VMEM((8, 8, 128), F32),
            pltpu.VMEM((8, 8, 128), F32),
            pltpu.VMEM((8, 8, 128), F32),
            pltpu.VMEM((8, 8, 128), F32),
            pltpu.VMEM((8, 8, 128), F32),
            dma((7,)), dma((7,)),
            dma((2, 7, 2)), dma((2, 7, 2)),
            dma((3,)), dma((3,)),
            dma((2, 4)), dma((2, 4)),
            dma((1,)), dma((1,)),
            dma((4, 7)), dma((4, 7)),
        ],
        compiler_params=pltpu.CompilerParams(
            collective_id=0, has_side_effects=True, vmem_limit_bytes=50 << 20
        ),
    )(packed, digits, head_weight, bounds)
    v = lax.axis_index("vocab")
    first = ((v % NC) * NX + (v // NC) % NX) * 16
    own = lax.dynamic_slice(final, (0, first), (2, 16))
    return (own[0], own[1], seq[0, : lengths.shape[0]] / lengths.astype(F32))


def solution(mesh):
    placed = (
        P("vocab", "width"),
        P("width"),
        P("vocab", "width"),
        P(("vocab", "width")),
        P(("vocab", "width")),
        P(),
    )
    return jax.shard_map(
        per_device,
        mesh=mesh,
        in_specs=placed,
        out_specs=(P(("vocab", "width")), P(("vocab", "width")), P()),
        check_vma=False,
    )
```

```python
import functools

import jax
import jax.numpy as jnp
from jax import lax
from jax.experimental import pallas as pl
from jax.experimental.pallas import tpu as pltpu
from jax.sharding import PartitionSpec as P

epsilon = 1e-06
MESH = pl.DeviceIdType.MESH
NX, NY, NC, NZ = 4, 8, 2, 8
GROUP = NC * NX
F32 = jnp.float32
NT = (((1,), (1,)), ((), ()))


def remote(src, dst, send, recv, device):
    return pltpu.make_async_remote_copy(
        src_ref=src, dst_ref=dst, send_sem=send, recv_sem=recv, device_id=device, device_id_type=MESH
    )


def merge_tiles(tiles):
    peak = functools.reduce(jnp.maximum, [t[0:1] for t in tiles])
    total = spread = target = None
    for t in tiles:
        gap = t[0:1] - peak
        lift = jnp.exp(gap)
        parts = (t[1:2] * lift, lift * (t[2:3] + gap * t[1:2]), t[3:4])
        if total is None:
            total, spread, target = parts
        else:
            total, spread, target = total + parts[0], spread + parts[1], target + parts[2]
    return peak, total, spread, target


def stack_rows(*rows):
    return jnp.concatenate(rows + (jnp.zeros((8 - len(rows), rows[0].shape[1]), F32),), axis=0)


def kernel(
    hidden, gain_row, digits, head, bounds, final, seq,
    raw, gains, toks, heads, acc, wanted, run, stats, got_y, got_c, sum_z, sum_y,
    az_s, az_r, g_s, g_r, h_s, h_r, x_s, x_r, y_s, y_r, c_s, c_r, t_s, t_r, own_s,
):
    v = lax.axis_index("vocab")
    w = lax.axis_index("width")
    core = v % NC
    x = (v // NC) % NX
    y = v // (NC * NX)
    mine = core * NX + x
    rows, wide = head.shape
    ways, parts = 2, 4
    half = rows // ways
    edges = [(half // 16 * i + parts - 1) // parts * 16 for i in range(parts)] + [half]

    def at_z(d):
        return {"width": (w + d) % NZ}

    def at_y(d):
        return {"vocab": (((y + d) % NY) * NX + x) * NC + core}

    def at_c(d):
        other = (mine + d) % GROUP
        return {"vocab": (y * NX + other % NX) * NC + other // NX}

    def at_x(d):
        return {"vocab": (y * NX + (x + d) % NX) * NC + core}

    barrier = pltpu.get_barrier_semaphore()
    for d in range(1, 8):
        for device in (at_z(d), at_y(d), at_c(d)):
            pl.semaphore_signal(barrier, inc=1, device_id=device, device_id_type=MESH)
    pl.semaphore_wait(barrier, 21)

    def rows_of(z):
        return hidden.at[pl.ds(pl.multiple_of(z * 16, 16), 16)]

    local = [
        pltpu.make_async_copy(rows_of(w), raw.at[w], own_s.at[0]),
        pltpu.make_async_copy(gain_row, gains.at[w], own_s.at[1]),
        pltpu.make_async_copy(head, heads.at[w], own_s.at[2]),
    ]
    for copy in local:
        copy.start()
    sent = []
    for d in range(1, NZ):
        to = (w + d) % NZ
        sent.append(remote(rows_of(to), raw.at[w], az_s.at[d - 1], az_r.at[d - 1], at_z(d)))
        sent.append(remote(gain_row, gains.at[w], g_s.at[d - 1], g_r.at[d - 1], at_z(d)))
    for copy in sent:
        copy.start()

    ring = {}

    def head_arrive(step, part):
        for way in range(ways):
            ring[step - 1, way, part].wait_recv()

    def rows_at(way, part):
        return way * half + edges[part], edges[part + 1] - edges[part]

    def head_step(step):
        for part in range(parts):
            for way in range(ways):
                if step > 0:
                    ring[step - 1, way, part].wait_recv()
                span = pl.ds(*rows_at(way, part))
                owner = (w - step + NZ) % NZ if way == 0 else (w + step) % NZ
                slab = heads.at[owner, span]
                copy = remote(
                    head.at[span] if step == 0 else slab,
                    slab,
                    h_s.at[way, step, part],
                    h_r.at[way, step, part],
                    at_z(1 if way == 0 else NZ - 1),
                )
                copy.start()
                ring[step, way, part] = copy

    head_step(0)
    acc[...] = jnp.zeros_like(acc)
    for copy in local:
        copy.wait()
    for copy in sent:
        copy.wait_recv()

    values = raw[...].astype(F32)
    gain = gains[...].astype(F32)
    energy = jnp.sum(jnp.sum(values * values, axis=0), axis=1, keepdims=True)
    inv = lax.rsqrt(energy / (wide * NZ) + epsilon)
    toks[y, mine, 0:NZ] = (values * inv[None] * gain).astype(jnp.bfloat16)
    toks[y, mine, NZ] = digits[...]

    spot = toks.at[y, mine]
    xs = []
    for d in range(1, NX):
        copy = remote(spot, spot, x_s.at[d - 1], x_r.at[d - 1], at_x(d))
        copy.start()
        xs.append(copy)
    for copy in xs:
        copy.wait_recv()

    yring = {}

    def y_step(step):
        for way, hops in ((0, NY // 2), (1, NY // 2 - 1)):
            if 0 < step <= hops:
                yring[step - 1, way].wait_recv()
            if step < hops:
                owner = (y - step + NY) % NY if way == 0 else (y + step) % NY
                block = toks.at[owner, pl.ds(core * NX, NX)]
                copy = remote(
                    block, block, y_s.at[way, step], y_r.at[way, step], at_y(1 if way == 0 else NY - 1)
                )
                copy.start()
                yring[step, way] = copy

    y_step(0)
    for step in range(1, NY // 2 + 1):
        head_step(step)
        y_step(step)
    side = toks.at[:, pl.ds(core * NX, NX)]
    cross = remote(side, side, c_s.at[0], c_r.at[0], {"vocab": v - core + (1 - core)})
    cross.start()

    def multiply(near, far, spans):
        def one(i, carry):
            step = near + i // 4
            tile = i % 4
            lanes = pl.ds(pl.multiple_of(tile * 256, 256), 256)
            for way in range(ways):
                owner = (w - step + NZ) % NZ if way == 0 else (w + step) % NZ
                tokens = toks[pl.ds(tile * 2, 2), :, owner].reshape(256, wide)
                span = pl.ds(*spans[way])
                acc[span, lanes] += lax.dot_general(
                    heads[owner, span], tokens, NT, preferred_element_type=F32
                )
            return carry

        lax.fori_loop(0, (far - near) * 4, one, 0)

    pick = (
        lax.broadcasted_iota(jnp.int32, (8, 256), 0) == lax.broadcasted_iota(jnp.int32, (8, 256), 1)
    ).astype(jnp.bfloat16)

    def side_values(block):
        return lax.dot_general(pick, block.reshape(128, 256), NT, preferred_element_type=F32)

    def note_wanted(tile, carry):
        extra = side_values(toks[tile, :, NZ])
        index = extra[0:1] * 4096.0 + extra[1:2] * 64.0 + extra[2:3] - (v * rows).astype(F32)
        wanted[tile] = jnp.broadcast_to(index, (8, 128)).astype(jnp.int32)
        return carry

    def summarize(part):
        def one(tile, carry):
            lanes = pl.ds(pl.multiple_of(tile * 128, 128), 128)
            chunks = []
            for way in range(ways):
                base, count = rows_at(way, part)
                chunks += [(base + i * (count // 2), count // 2) for i in range(2)]

            def block(base, count):
                return acc[pl.ds(base, count), lanes].reshape(count // 8, 8, 128)

            peak = functools.reduce(jnp.maximum, [jnp.max(block(*c), axis=0) for c in chunks])
            target = wanted[tile] - lax.broadcasted_iota(jnp.int32, (8, 128), 0)
            sums = [jnp.zeros((8, 128), F32)] * 3
            if part > 0:
                before = run[tile, 0]
                peak = jnp.maximum(before, peak)
                gap = before - peak
                lift = jnp.exp(gap)
                sums = [
                    run[tile, 1] * lift,
                    lift * (run[tile, 2] + gap * run[tile, 1]),
                    run[tile, 3],
                ]
            for base, count in chunks:
                logits = block(base, count)
                shifted = logits - peak[None]
                weights = jnp.exp(shifted)
                place = lax.broadcasted_iota(jnp.int32, logits.shape, 0) * 8 + base
                hit = jnp.where(place == target[None], logits, 0.0)
                sums = [
                    sums[0] + jnp.sum(weights, axis=0),
                    sums[1] + jnp.sum(weights * shifted, axis=0),
                    sums[2] + jnp.sum(hit, axis=0),
                ]
            run[tile, 0] = peak
            for k in range(3):
                run[tile, k + 1] = sums[k]
            return carry

        lax.fori_loop(0, NY, one, 0)

    def close():
        for tile in range(NY):
            peak = jnp.max(run[tile, 0], axis=0, keepdims=True)
            gap = run[tile, 0] - peak
            lift = jnp.exp(gap)
            rest = (run[tile, 1] * lift, lift * (run[tile, 2] + gap * run[tile, 1]), run[tile, 3])
            stats[tile] = stack_rows(peak, *[jnp.sum(t, axis=0, keepdims=True) for t in rest])

    whole = [(way * half, half) for way in range(ways)]
    head_step(5)
    cross.wait_recv()
    lax.fori_loop(0, NY, note_wanted, 0)
    multiply(0, 3, whole)
    head_step(6)
    multiply(3, 7, whole)
    for part in range(parts):
        head_arrive(7, part)
        multiply(7, 8, [rows_at(way, part) for way in range(ways)])
        summarize(part)
    close()

    def swap(stage, buffer, own, at, source=None):
        copies = []
        for d in range(1, 8):
            src = buffer.at[own] if source is None else source((own + d) % 8)
            copy = remote(src, buffer.at[own], t_s.at[stage, d - 1], t_r.at[stage, d - 1], at(d))
            copy.start()
            copies.append(copy)
        for copy in copies:
            copy.wait_recv()
        return copies

    done = []
    got_y[y] = stats[y]
    done += swap(0, got_y, y, at_y, lambda i: stats.at[i])
    got_c[mine] = stack_rows(*merge_tiles([got_y[i] for i in range(8)]))
    done += swap(1, got_c, mine, at_c)
    peak, total, spread, target = merge_tiles([got_c[i] for i in range(8)])

    kept = side_values(toks[y, :, NZ])[3:4]
    log_total = jnp.log(total)
    entropy = kept * (log_total - spread / total)
    logprob = kept * (target - peak - log_total)
    final[...] = stack_rows(entropy, logprob)

    lane = lax.broadcasted_iota(jnp.int32, (128, 128), 1)
    slot = lane // 16
    token = ((((y * NX + slot % NX) * NC + slot // NX) * NZ) + w) * 16 + lane % 16
    member = ((token >= bounds[0]) & (token < bounds[1])).astype(F32)
    sum_z[w] = lax.dot_general(
        stack_rows(logprob), member, NT, precision=lax.Precision.HIGHEST, preferred_element_type=F32
    )
    done += swap(2, sum_z, w, at_z)
    sum_y[y] = functools.reduce(jnp.add, [sum_z[i] for i in range(8)])
    done += swap(3, sum_y, y, at_y)
    seq[...] = functools.reduce(jnp.add, [sum_y[i] for i in range(8)])

    for copy in sent + xs + [cross] + done + list(yring.values()) + list(ring.values()):
        copy.wait_send()


def per_device(hidden, norm_gain, head_weight, targets, pad_mask, lengths):
    rows, wide = head_weight.shape
    columns = jnp.stack([targets // 4096, (targets // 64) % 64, targets % 64, pad_mask], axis=1)
    digits = jnp.pad(columns.astype(jnp.bfloat16), ((0, 0), (0, wide - 4)))
    seq_ends = jnp.cumsum(lengths)
    bounds = jnp.pad(jnp.stack([seq_ends - lengths, seq_ends]), ((0, 0), (0, 128 - lengths.shape[0])))
    bounds = jnp.broadcast_to(bounds[:, :, None], (2, 128, 128))
    vmem = pl.BlockSpec(memory_space=pltpu.VMEM)
    hbm = pl.BlockSpec(memory_space=pl.ANY)
    dma = pltpu.SemaphoreType.DMA
    bf = jnp.bfloat16
    final, seq = pl.pallas_call(
        kernel,
        out_shape=(jax.ShapeDtypeStruct((8, 128), F32), jax.ShapeDtypeStruct((8, 128), F32)),
        in_specs=[hbm, hbm, vmem, hbm, vmem],
        out_specs=(vmem, vmem),
        scratch_shapes=[
            pltpu.VMEM((NZ, 16, wide), bf),
            pltpu.VMEM((NZ, 1, wide), bf),
            pltpu.VMEM((NY, GROUP, NZ + 1, 16, wide), bf),
            pltpu.VMEM((NZ, rows, wide), bf),
            pltpu.VMEM((rows, 1024), F32),
            pltpu.VMEM((NY, 8, 128), jnp.int32),
            pltpu.VMEM((NY, 4, 8, 128), F32),
            pltpu.VMEM((8, 8, 128), F32),
            pltpu.VMEM((8, 8, 128), F32),
            pltpu.VMEM((8, 8, 128), F32),
            pltpu.VMEM((8, 8, 128), F32),
            pltpu.VMEM((8, 8, 128), F32),
            dma((7,)), dma((7,)),
            dma((7,)), dma((7,)),
            dma((2, 7, 4)), dma((2, 7, 4)),
            dma((3,)), dma((3,)),
            dma((2, 4)), dma((2, 4)),
            dma((1,)), dma((1,)),
            dma((4, 7)), dma((4, 7)),
            dma((3,)),
        ],
        compiler_params=pltpu.CompilerParams(
            collective_id=0, has_side_effects=True, vmem_limit_bytes=50 << 20
        ),
    )(hidden, norm_gain[None], digits, head_weight, bounds)
    v = lax.axis_index("vocab")
    first = ((v % NC) * NX + (v // NC) % NX) * 16
    own = lax.dynamic_slice(final, (0, first), (2, 16))
    return (own[0], own[1], seq[0, : lengths.shape[0]] / lengths.astype(F32))


def solution(mesh):
    placed = (
        P("vocab", "width"),
        P("width"),
        P("vocab", "width"),
        P(("vocab", "width")),
        P(("vocab", "width")),
        P(),
    )
    return jax.shard_map(
        per_device,
        mesh=mesh,
        in_specs=placed,
        out_specs=(P(("vocab", "width")), P(("vocab", "width")), P()),
        check_vma=False,
    )
```

```python
import functools

import jax
import jax.numpy as jnp
from jax import lax
from jax.experimental import pallas as pl
from jax.experimental.pallas import tpu as pltpu
from jax.sharding import PartitionSpec as P

epsilon = 1e-06
MESH = pl.DeviceIdType.MESH
NX, NY, NC, NZ = 4, 8, 2, 8
GROUP = NC * NX
F32 = jnp.float32
NT = (((1,), (1,)), ((), ()))


def remote(src, dst, send, recv, device):
    return pltpu.make_async_remote_copy(
        src_ref=src, dst_ref=dst, send_sem=send, recv_sem=recv, device_id=device, device_id_type=MESH
    )


def merge_tiles(tiles):
    peak = functools.reduce(jnp.maximum, [t[0:1] for t in tiles])
    total = spread = target = None
    for t in tiles:
        gap = t[0:1] - peak
        lift = jnp.exp(gap)
        parts = (t[1:2] * lift, lift * (t[2:3] + gap * t[1:2]), t[3:4])
        if total is None:
            total, spread, target = parts
        else:
            total, spread, target = total + parts[0], spread + parts[1], target + parts[2]
    return peak, total, spread, target


def stack_rows(*rows):
    return jnp.concatenate(rows + (jnp.zeros((8 - len(rows), rows[0].shape[1]), F32),), axis=0)


def kernel(
    hidden, gain_row, digits, head, bounds, final, seq,
    raw, gains, toks, heads, acc, wanted, run, stats, got_y, got_c, sum_z, sum_y,
    az_s, az_r, g_s, g_r, h_s, h_r, x_s, x_r, y_s, y_r, c_s, c_r, t_s, t_r, own_s,
):
    v = lax.axis_index("vocab")
    w = lax.axis_index("width")
    core = v % NC
    x = (v // NC) % NX
    y = v // (NC * NX)
    mine = core * NX + x
    rows, wide = head.shape
    ways, parts = 2, 4
    half = rows // ways
    edges = [(half // 16 * i + parts - 1) // parts * 16 for i in range(parts)] + [half]

    def at_z(d):
        return {"width": (w + d) % NZ}

    def at_y(d):
        return {"vocab": (((y + d) % NY) * NX + x) * NC + core}

    def at_c(d):
        other = (mine + d) % GROUP
        return {"vocab": (y * NX + other % NX) * NC + other // NX}

    def at_x(d):
        return {"vocab": (y * NX + (x + d) % NX) * NC + core}

    barrier = pltpu.get_barrier_semaphore()
    for d in range(1, 8):
        for device in (at_z(d), at_y(d), at_c(d)):
            pl.semaphore_signal(barrier, inc=1, device_id=device, device_id_type=MESH)
    pl.semaphore_wait(barrier, 21)

    def rows_of(z):
        return hidden.at[pl.ds(pl.multiple_of(z * 16, 16), 16)]

    local = [
        pltpu.make_async_copy(rows_of(w), raw.at[w], own_s.at[0]),
        pltpu.make_async_copy(gain_row, gains.at[w], own_s.at[1]),
        pltpu.make_async_copy(head, heads.at[w], own_s.at[2]),
    ]
    for copy in local:
        copy.start()
    sent = []
    for d in range(1, NZ):
        to = (w + d) % NZ
        sent.append(remote(rows_of(to), raw.at[w], az_s.at[d - 1], az_r.at[d - 1], at_z(d)))
        sent.append(remote(gain_row, gains.at[w], g_s.at[d - 1], g_r.at[d - 1], at_z(d)))
    for copy in sent:
        copy.start()

    ring = {}

    def head_arrive(step, part):
        for way in range(ways):
            ring[step - 1, way, part].wait_recv()

    def rows_at(way, part):
        return way * half + edges[part], edges[part + 1] - edges[part]

    def head_step(step):
        for part in range(parts):
            for way in range(ways):
                if step > 0:
                    ring[step - 1, way, part].wait_recv()
                span = pl.ds(*rows_at(way, part))
                owner = (w - step + NZ) % NZ if way == 0 else (w + step) % NZ
                slab = heads.at[owner, span]
                copy = remote(
                    head.at[span] if step == 0 else slab,
                    slab,
                    h_s.at[way, step, part],
                    h_r.at[way, step, part],
                    at_z(1 if way == 0 else NZ - 1),
                )
                copy.start()
                ring[step, way, part] = copy

    head_step(0)
    acc[...] = jnp.zeros_like(acc)
    for copy in local:
        copy.wait()
    for copy in sent:
        copy.wait_recv()

    values = raw[...].astype(F32)
    gain = gains[...].astype(F32)
    energy = jnp.sum(jnp.sum(values * values, axis=0), axis=1, keepdims=True)
    inv = lax.rsqrt(energy / (wide * NZ) + epsilon)
    toks[y, mine, 0:NZ] = (values * inv[None] * gain).astype(jnp.bfloat16)
    toks[y, mine, NZ] = digits[...]

    spot = toks.at[y, mine]
    xs = []
    for d in range(1, NX):
        copy = remote(spot, spot, x_s.at[d - 1], x_r.at[d - 1], at_x(d))
        copy.start()
        xs.append(copy)
    head_step(1)
    for copy in xs:
        copy.wait_recv()

    yring = {}
    cross = []

    def cross_block(owner):
        block = toks.at[owner, pl.ds(core * NX, NX)]
        k = len(cross)
        copy = remote(block, block, c_s.at[k], c_r.at[k], {"vocab": v - core + (1 - core)})
        copy.start()
        cross.append(copy)

    def y_step(step):
        for way, hops in ((0, NY // 2), (1, NY // 2 - 1)):
            if 0 < step <= hops:
                yring[step - 1, way].wait_recv()
            if step < hops:
                owner = (y - step + NY) % NY if way == 0 else (y + step) % NY
                block = toks.at[owner, pl.ds(core * NX, NX)]
                copy = remote(
                    block, block, y_s.at[way, step], y_r.at[way, step], at_y(1 if way == 0 else NY - 1)
                )
                copy.start()
                yring[step, way] = copy
            if step <= hops and (step > 0 or way == 0):
                cross_block((y - step + NY) % NY if way == 0 else (y + step) % NY)

    y_step(0)
    for step in range(1, NY // 2 + 1):
        head_step(step + 1)
        y_step(step)
    def multiply(near, far, spans):
        def one(i, carry):
            step = near + i // 4
            tile = i % 4
            lanes = pl.ds(pl.multiple_of(tile * 256, 256), 256)
            for way in range(ways):
                owner = (w - step + NZ) % NZ if way == 0 else (w + step) % NZ
                tokens = toks[pl.ds(tile * 2, 2), :, owner].reshape(256, wide)
                span = pl.ds(*spans[way])
                acc[span, lanes] += lax.dot_general(
                    heads[owner, span], tokens, NT, preferred_element_type=F32
                )
            return carry

        lax.fori_loop(0, (far - near) * 4, one, 0)

    pick = (
        lax.broadcasted_iota(jnp.int32, (8, 256), 0) == lax.broadcasted_iota(jnp.int32, (8, 256), 1)
    ).astype(jnp.bfloat16)

    def side_values(block):
        return lax.dot_general(pick, block.reshape(128, 256), NT, preferred_element_type=F32)

    def note_wanted(tile, carry):
        extra = side_values(toks[tile, :, NZ])
        index = extra[0:1] * 4096.0 + extra[1:2] * 64.0 + extra[2:3] - (v * rows).astype(F32)
        wanted[tile] = jnp.broadcast_to(index, (8, 128)).astype(jnp.int32)
        return carry

    def summarize(part):
        def one(tile, carry):
            lanes = pl.ds(pl.multiple_of(tile * 128, 128), 128)
            chunks = []
            for way in range(ways):
                base, count = rows_at(way, part)
                chunks += [(base + i * (count // 2), count // 2) for i in range(2)]

            def block(base, count):
                return acc[pl.ds(base, count), lanes].reshape(count // 8, 8, 128)

            peak = functools.reduce(jnp.maximum, [jnp.max(block(*c), axis=0) for c in chunks])
            target = wanted[tile] - lax.broadcasted_iota(jnp.int32, (8, 128), 0)
            sums = [jnp.zeros((8, 128), F32)] * 3
            if part > 0:
                before = run[tile, 0]
                peak = jnp.maximum(before, peak)
                gap = before - peak
                lift = jnp.exp(gap)
                sums = [
                    run[tile, 1] * lift,
                    lift * (run[tile, 2] + gap * run[tile, 1]),
                    run[tile, 3],
                ]
            for base, count in chunks:
                logits = block(base, count)
                shifted = logits - peak[None]
                weights = jnp.exp(shifted)
                place = lax.broadcasted_iota(jnp.int32, logits.shape, 0) * 8 + base
                hit = jnp.where(place == target[None], logits, 0.0)
                sums = [
                    sums[0] + jnp.sum(weights, axis=0),
                    sums[1] + jnp.sum(weights * shifted, axis=0),
                    sums[2] + jnp.sum(hit, axis=0),
                ]
            run[tile, 0] = peak
            for k in range(3):
                run[tile, k + 1] = sums[k]
            return carry

        lax.fori_loop(0, NY, one, 0)

    def close():
        for tile in range(NY):
            peak = jnp.max(run[tile, 0], axis=0, keepdims=True)
            gap = run[tile, 0] - peak
            lift = jnp.exp(gap)
            rest = (run[tile, 1] * lift, lift * (run[tile, 2] + gap * run[tile, 1]), run[tile, 3])
            stats[tile] = stack_rows(peak, *[jnp.sum(t, axis=0, keepdims=True) for t in rest])

    whole = [(way * half, half) for way in range(ways)]
    for copy in cross:
        copy.wait_recv()
    lax.fori_loop(0, NY, note_wanted, 0)
    multiply(0, 3, whole)
    head_step(6)
    multiply(3, 7, whole)
    for part in range(parts):
        head_arrive(7, part)
        multiply(7, 8, [rows_at(way, part) for way in range(ways)])
        summarize(part)
    close()

    def swap(stage, buffer, own, at, source=None):
        copies = []
        for d in range(1, 8):
            src = buffer.at[own] if source is None else source((own + d) % 8)
            copy = remote(src, buffer.at[own], t_s.at[stage, d - 1], t_r.at[stage, d - 1], at(d))
            copy.start()
            copies.append(copy)
        for copy in copies:
            copy.wait_recv()
        return copies

    done = []
    got_y[y] = stats[y]
    done += swap(0, got_y, y, at_y, lambda i: stats.at[i])
    got_c[mine] = stack_rows(*merge_tiles([got_y[i] for i in range(8)]))
    done += swap(1, got_c, mine, at_c)
    peak, total, spread, target = merge_tiles([got_c[i] for i in range(8)])

    kept = side_values(toks[y, :, NZ])[3:4]
    log_total = jnp.log(total)
    entropy = kept * (log_total - spread / total)
    logprob = kept * (target - peak - log_total)
    final[...] = stack_rows(entropy, logprob)

    lane = lax.broadcasted_iota(jnp.int32, (128, 128), 1)
    slot = lane // 16
    token = ((((y * NX + slot % NX) * NC + slot // NX) * NZ) + w) * 16 + lane % 16
    member = ((token >= bounds[0]) & (token < bounds[1])).astype(F32)
    sum_z[w] = lax.dot_general(
        stack_rows(logprob), member, NT, precision=lax.Precision.HIGHEST, preferred_element_type=F32
    )
    done += swap(2, sum_z, w, at_z)
    sum_y[y] = functools.reduce(jnp.add, [sum_z[i] for i in range(8)])
    done += swap(3, sum_y, y, at_y)
    seq[...] = functools.reduce(jnp.add, [sum_y[i] for i in range(8)])

    for copy in sent + xs + cross + done + list(yring.values()) + list(ring.values()):
        copy.wait_send()


def per_device(hidden, norm_gain, head_weight, targets, pad_mask, lengths):
    rows, wide = head_weight.shape
    columns = jnp.stack([targets // 4096, (targets // 64) % 64, targets % 64, pad_mask], axis=1)
    digits = jnp.pad(columns.astype(jnp.bfloat16), ((0, 0), (0, wide - 4)))
    seq_ends = jnp.cumsum(lengths)
    bounds = jnp.pad(jnp.stack([seq_ends - lengths, seq_ends]), ((0, 0), (0, 128 - lengths.shape[0])))
    bounds = jnp.broadcast_to(bounds[:, :, None], (2, 128, 128))
    vmem = pl.BlockSpec(memory_space=pltpu.VMEM)
    hbm = pl.BlockSpec(memory_space=pl.ANY)
    dma = pltpu.SemaphoreType.DMA
    bf = jnp.bfloat16
    final, seq = pl.pallas_call(
        kernel,
        out_shape=(jax.ShapeDtypeStruct((8, 128), F32), jax.ShapeDtypeStruct((8, 128), F32)),
        in_specs=[hbm, hbm, vmem, hbm, vmem],
        out_specs=(vmem, vmem),
        scratch_shapes=[
            pltpu.VMEM((NZ, 16, wide), bf),
            pltpu.VMEM((NZ, 1, wide), bf),
            pltpu.VMEM((NY, GROUP, NZ + 1, 16, wide), bf),
            pltpu.VMEM((NZ, rows, wide), bf),
            pltpu.VMEM((rows, 1024), F32),
            pltpu.VMEM((NY, 8, 128), jnp.int32),
            pltpu.VMEM((NY, 4, 8, 128), F32),
            pltpu.VMEM((8, 8, 128), F32),
            pltpu.VMEM((8, 8, 128), F32),
            pltpu.VMEM((8, 8, 128), F32),
            pltpu.VMEM((8, 8, 128), F32),
            pltpu.VMEM((8, 8, 128), F32),
            dma((7,)), dma((7,)),
            dma((7,)), dma((7,)),
            dma((2, 7, 4)), dma((2, 7, 4)),
            dma((3,)), dma((3,)),
            dma((2, 4)), dma((2, 4)),
            dma((8,)), dma((8,)),
            dma((4, 7)), dma((4, 7)),
            dma((3,)),
        ],
        compiler_params=pltpu.CompilerParams(
            collective_id=0, has_side_effects=True, vmem_limit_bytes=50 << 20
        ),
    )(hidden, norm_gain[None], digits, head_weight, bounds)
    v = lax.axis_index("vocab")
    first = ((v % NC) * NX + (v // NC) % NX) * 16
    own = lax.dynamic_slice(final, (0, first), (2, 16))
    return (own[0], own[1], seq[0, : lengths.shape[0]] / lengths.astype(F32))


def solution(mesh):
    placed = (
        P("vocab", "width"),
        P("width"),
        P("vocab", "width"),
        P(("vocab", "width")),
        P(("vocab", "width")),
        P(),
    )
    return jax.shard_map(
        per_device,
        mesh=mesh,
        in_specs=placed,
        out_specs=(P(("vocab", "width")), P(("vocab", "width")), P()),
        check_vma=False,
    )
```
